256 devices in a mesh: expert: 32 (over z_lo, x, core), dp: 8 (over z_hi, y).
Axes of the slice: x: 4, y: 4, z: 8 (z_hi: 2, z_lo: 4; z = z_hi * 4 + z_lo), core: 2. Of those that a mesh axis runs over, the one named last changes fastest.
Arguments:
- tokens: bfloat16 [32768, 2048], P(('expert', 'dp')), may hold values from -6 to 6
- w_router: bfloat16 [2048, 32], replicated, may hold values from -0.125 to 0.125
- w_up: bfloat16 [32, 2048, 7168], P('expert', None, 'dp'), may hold values from -0.125 to 0.125
- w_down: bfloat16 [32, 7168, 2048], P('expert', 'dp'), may hold values from -0.0625 to 0.0625
- norm_gain: float32 [2048], replicated, may hold values from 0.25 to 1.75
- readout: bfloat16 [2048, 128], replicated, may hold values from -0.125 to 0.125
- expert_ids: int32 [32768, 2], P(('expert', 'dp')), may hold values from 0 to 31, all different within a row; in each aligned block of 128 rows (0 to 127, 128 to 255, ...) at most 8 rows name the same one
- substation_ids: int32 [32768], P(('expert', 'dp')), may hold values from 0 to 255
- hour_index: int32 [32768], P(('expert', 'dp')), may hold values from 0 to 7
- target: float32 [2048, 128], replicated, may hold values from -24 to 24
Outputs:
- load_table: float32 [2048, 128], P(('expert', 'dp'))
- loss_value: float32 [], replicated
- grad_down: bfloat16 [32, 7168, 2048], P('expert', 'dp')
The draws below stay inside these ranges and needn't reach their ends.
Inputs may be any that keep to these rules, and one draw needn't show every extreme that they name: `expert_ids`: each row names two different experts; among the 128 rows of one device every expert is named exactly 8 times.
All inputs are finite; a program needn't handle non-finite values.
Results may differ from the reference program's by a relative error of at most 0.0075.
Values may be sent and summed in bfloat16 or wider, within the bound.
No kernel may reach another device: no remote copies, remote signals or barrier semaphores. Data moves between devices by JAX's collectives and lax.ppermute only.
A program may use at most 128 MiB of HBM per device.

```python
import math
import jax
import jax.numpy as jnp
import numpy as np
from jax import lax

D = 2048
FF = 7168
Q = 128
HOURS = 8
TOK_DEV = 128
EXPERTS = 32
CAP = 8
FD = 896
TOKENS = 32768
KEYS = 2048
SUBS = 256
N_EXPERT = 32
N_DP = 8


def touch_ends(array, rng, least, top_value):
    dims = array.shape
    spot = [jax.random.randint(jax.random.fold_in(rng, axis), (), 0, dims[axis]) for axis in range(len(dims))]
    array = array.at[tuple(spot)].set(least)
    longest = dims.index(max(dims))
    spot[longest] = (spot[longest] + 1) % dims[longest]
    return array.at[tuple(spot)].set(top_value)


def block_scale(key, extent, shards, smallest, high):
    factor_of = 1.0
    for dim, shards_of in shards:
        steps = jax.random.uniform(jax.random.fold_in(jax.random.fold_in(key, 6), dim), (shards_of,), jnp.float32, smallest / len(shards), high / len(shards))
        factor_of = factor_of * jnp.repeat(jnp.exp(steps), extent[dim] // shards_of).reshape((-1,) + (1,) * (len(extent) - 1 - dim))
    return factor_of


def deal_out(stream_key, own, number, rows, number_of, top, reach, slope):
    order = jax.random.permutation(stream_key, number_of)
    packed, ordinary = portions_of(number_of, rows * top, reach, slope, True), portions_of(number_of, rows * top, reach, slope, False)
    places = jnp.arange(number_of)

    def named(sizes, turn):
        used = int((sizes > 0).sum())
        fixed = max(1, used // 4)
        shifted = fixed + (places - fixed + turn * (used - fixed)) % max(1, number_of - fixed)
        return jnp.zeros((number_of,), jnp.int32).at[order[jnp.where(places < fixed, places, shifted)]].set(jnp.asarray(sizes, jnp.int32))

    sizes = jnp.where(number % 4 == 0, named(packed, number // 4), named(ordinary, number - number // 4 - 1))
    mixed = jax.random.permutation(jax.random.fold_in(own, 3), number_of)
    giver, taker = mixed[0:number_of // 2 * 2:2], mixed[1:number_of // 2 * 2:2]
    room = jnp.minimum(sizes[giver] - 1, reach - sizes[taker]) // 2
    room = jnp.where((giver == order[0]) | (taker == order[0]) | (sizes[taker] == 0), 0, jnp.maximum(room, 0))
    shifted = jax.random.randint(jax.random.fold_in(own, 4), (number_of // 2,), 0, 1 << 20) % (room + 1)
    sizes = sizes.at[giver].add(-shifted).at[taker].add(shifted)
    members = jnp.searchsorted(jnp.cumsum(sizes), jnp.arange(rows * top), side="right").astype(jnp.int32)
    grid = members.reshape(top, rows).T
    grid = grid[jax.random.permutation(jax.random.fold_in(own, 1), rows)]
    turn = jax.random.randint(jax.random.fold_in(own, 2), (rows, 1), 0, top)
    return jnp.take_along_axis(grid, (jnp.arange(top)[None, :] + turn) % top, axis=1)


def portions_of(amount, total, limit, skew, full):
    portions = [(1 << 20) // math.isqrt(standing ** skew) + 1 for standing in range(1, amount + 1)]
    largest = limit if full else min(limit, max(-(-total // amount), total * portions[0] // sum(portions)))
    least = 1 if total - largest >= amount - 1 else 0
    counts, rest = [largest] + [least] * (amount - 1), total - largest - least * (amount - 1)
    while rest > 0:
        movable = [i for i in range(1, amount) if counts[i] < largest] or [i for i in range(1, amount) if counts[i] < limit]
        pool, left = sum([portions[i] for i in movable]), rest
        for i in movable:
            extra = min(limit - counts[i], max(1, left * portions[i] // pool), rest)
            counts[i] = counts[i] + extra
            rest = rest - extra
    return np.array(counts)


def centred(own_key, extent, deviation, limit, cuts=(), kind=jnp.bfloat16):
    level = block_scale(own_key, extent, cuts, -0.22, 0.18) if cuts else 1.0
    entries = jax.random.normal(own_key, extent, jnp.float32) * deviation * level
    return jnp.minimum(jnp.maximum(entries, -limit), limit).astype(kind)


def setup_inputs(seed: int = 0) -> dict:
    key_of = jax.random.split(jax.random.key(seed), 11)
    tokens = centred(key_of[0], (TOKENS, D), 1.0, 6.0, ((0, 256),))
    w_router = centred(key_of[1], (D, EXPERTS), D ** -0.5, 0.125)
    w_up = centred(key_of[2], (EXPERTS, D, FF), D ** -0.5, 0.125, ((0, 32), (2, 8)))
    w_down = centred(key_of[3], (EXPERTS, FF, D), FF ** -0.5, 0.0625, ((0, 32), (1, 8)))
    norm_gain = jnp.clip(1.0 + 0.15 * jax.random.normal(key_of[4], (D,), jnp.float32), 0.25, 1.75)
    readout = centred(key_of[5], (D, Q), D ** -0.5, 0.125)
    expert_ids_keys = jax.random.split(jax.random.fold_in(key_of[6], 1), TOKENS // TOK_DEV)
    expert_ids_turns = jax.random.permutation(jax.random.fold_in(key_of[6], 3), TOKENS // TOK_DEV)
    expert_ids = jax.vmap(lambda own, number: deal_out(jax.random.fold_in(key_of[6], 2), own, number, TOK_DEV, EXPERTS, 2, CAP, 2))(expert_ids_keys, expert_ids_turns).reshape((TOKENS, 2))
    substation_ids = touch_ends(jax.random.randint(key_of[7], (TOKENS,), 0, SUBS), jax.random.fold_in(key_of[7], 1), 0, SUBS - 1).astype(jnp.int32)
    hour_index = touch_ends(jax.random.randint(key_of[8], (TOKENS,), 0, HOURS), jax.random.fold_in(key_of[8], 1), 0, HOURS - 1).astype(jnp.int32)
    target = centred(key_of[9], (KEYS, Q), 4.0, 24.0, (), jnp.float32)
    return {"tokens": tokens, "w_router": w_router, "w_up": w_up, "w_down": w_down, "norm_gain": norm_gain, "readout": readout, "expert_ids": expert_ids, "substation_ids": substation_ids, "hour_index": hour_index, "target": target}


def lift_rows(buffer_rows, up_matrix):
    return jax.nn.gelu(jnp.dot(buffer_rows, up_matrix, preferred_element_type=jnp.float32)).astype(jnp.bfloat16)

def reference(tokens, w_router, w_up, w_down, norm_gain, readout, expert_ids, substation_ids, hour_index, target):
    n_devices = N_EXPERT * N_DP
    flat_expert = expert_ids.reshape(-1).astype(jnp.int32)
    per_device = flat_expert.reshape(n_devices, 2 * TOK_DEV)
    one_hot = (per_device[:, :, None] == jnp.arange(EXPERTS, dtype=jnp.int32)[None, None, :]).astype(jnp.int32)
    position = lax.optimization_barrier(jnp.sum((jnp.cumsum(one_hot, axis=1) - 1) * one_hot, axis=2))
    device_row = jnp.arange(n_devices, dtype=jnp.int32)[:, None]
    flat_slot = (device_row * CAP + position).reshape(-1).astype(jnp.int32)
    depth = n_devices * CAP
    doubled = jnp.repeat(tokens, 2, axis=0)
    buffer = jnp.zeros((EXPERTS, depth, D), jnp.bfloat16).at[flat_expert, flat_slot].set(doubled)

    def forward(operands):
        buffer_rows, up_matrix, down_matrix = operands
        hidden = lift_rows(buffer_rows, up_matrix)
        parts = jnp.einsum('mdf,dfo->mdo', hidden.reshape(depth, N_DP, FD).astype(jnp.float32), down_matrix.reshape(N_DP, FD, D).astype(jnp.float32), precision=lax.Precision.HIGHEST)
        rounded = lax.optimization_barrier(parts.astype(jnp.bfloat16))
        return lax.optimization_barrier(jnp.sum(rounded.astype(jnp.float32), axis=1)).astype(jnp.bfloat16)
    expert_out = lax.map(forward, (buffer, w_up, w_down))
    per_token = expert_out[flat_expert, flat_slot].reshape(TOKENS, 2, D).astype(jnp.float32)
    logits = jnp.dot(tokens, w_router, preferred_element_type=jnp.float32)
    chosen = jnp.take_along_axis(logits, expert_ids.astype(jnp.int32), axis=1)
    gate_first = jax.nn.sigmoid(chosen[:, 0] - chosen[:, 1])
    gate_weights = jnp.stack([gate_first, 1.0 - gate_first], axis=1)
    mixed = tokens.astype(jnp.float32) + lax.optimization_barrier(jnp.sum(gate_weights[:, :, None] * per_token, axis=1))
    rscale = 1.0 / jnp.sqrt(lax.optimization_barrier(jnp.mean(mixed * mixed, axis=1, keepdims=True)) + 1e-05)
    normed = (mixed * rscale * norm_gain[None, :]).astype(jnp.bfloat16)
    loads = jnp.dot(normed, readout, preferred_element_type=jnp.float32)
    keys = (substation_ids * HOURS + hour_index).astype(jnp.int32)
    load_table = jax.ops.segment_sum(loads, keys, num_segments=KEYS)
    diff = load_table - target
    loss_value = 0.5 * jnp.mean(diff * diff)
    g_loads = diff[keys].astype(jnp.bfloat16)
    g_normed = jnp.dot(g_loads, readout.T, preferred_element_type=jnp.float32)
    scaled = g_normed * norm_gain[None, :]
    g_mixed = rscale * scaled - rscale ** 3 * mixed * lax.optimization_barrier(jnp.mean(scaled * mixed, axis=1, keepdims=True))
    g_assign = (gate_weights[:, :, None] * g_mixed[:, None, :]).astype(jnp.bfloat16).reshape(-1, D)
    g_buffer = jnp.zeros((EXPERTS, depth, D), jnp.bfloat16).at[flat_expert, flat_slot].set(g_assign)

    def backward(operands):
        buffer_rows, up_matrix, grad_rows = operands
        hidden = lift_rows(buffer_rows, up_matrix)
        return jnp.dot(hidden.T, grad_rows, preferred_element_type=jnp.float32).astype(jnp.bfloat16)
    grad_down = lax.map(backward, (buffer, w_up, g_buffer))
    return (load_table, loss_value, grad_down)
```

```python
import jax
import jax.numpy as jnp
from jax import lax
from jax.sharding import Mesh, PartitionSpec as P

HOURS = 8
BF = jnp.bfloat16
F32 = jnp.float32
EXP = ("zl", "x", "c")
WIDE = ("zl", "x", "c", "zh")
DP = ("zh", "y")
ALL = ("zl", "x", "c", "zh", "y")
HALVES = 2


def exchange(x, axes):
    return lax.all_to_all(x, axes, split_axis=0, concat_axis=0, tiled=True)


def up_one(x):
    return lax.ppermute(x, "y", [(i, (i + 1) % 4) for i in range(4)])


def down_one(x):
    return lax.ppermute(x, "y", [(i, (i + 3) % 4) for i in range(4)])


def ring_gather(own):
    half = own.shape[0] // 2
    prev = up_one(own)
    nxt = down_one(own)
    far_a = up_one(prev[:half])
    far_b = down_one(nxt[half:])
    return own, prev, nxt, far_a, far_b


def ring_scatter(own, prev, nxt, far):
    half = own.shape[0] // 2
    got_a = up_one(far[:half].astype(BF))
    got_b = down_one(far[half:].astype(BF))
    to_next = jnp.concatenate([(nxt[:half] + got_a).astype(BF), nxt[half:].astype(BF)], axis=0)
    to_prev = jnp.concatenate([prev[:half].astype(BF), (prev[half:] + got_b).astype(BF)], axis=0)
    from_prev = up_one(to_next)
    from_next = down_one(to_prev)
    return (own + from_prev.astype(F32) + from_next.astype(F32)).astype(BF)


def local(
    tokens,
    w_router,
    w_up,
    w_down,
    norm_gain,
    readout,
    expert_ids,
    substation_ids,
    hour_index,
    target,
):
    n_expert, n_all = 32, 256
    rows, width = tokens.shape
    cap = 2 * rows // n_expert
    slots = n_expert * cap
    cols = width // HALVES
    up_local, down_local = w_up[0], w_down[0]
    flat_expert = expert_ids.reshape(-1)
    one_hot = (flat_expert[:, None] == jnp.arange(n_expert, dtype=jnp.int32)[None, :]).astype(
        jnp.int32
    )
    position = jnp.sum((jnp.cumsum(one_hot, axis=0) - 1) * one_hot, axis=1)
    slot_index = flat_expert * cap + position
    slot_hot = (slot_index[:, None] == jnp.arange(slots, dtype=jnp.int32)[None, :]).astype(F32)
    slot_pairs = slot_hot.reshape(rows, 2, slots)
    placing = jnp.sum(slot_pairs, axis=1)
    placing_b = placing.astype(BF)
    placing_2 = jnp.broadcast_to(
        placing_b.reshape(rows, n_expert, 1, cap), (rows, n_expert, 2, cap)
    ).reshape(rows, 2 * slots)

    def send_rows(values):
        got = lax.dot_general(
            placing_2, values, (((0,), (0,)), ((), ())), preferred_element_type=F32
        )
        return exchange(got.astype(BF).reshape(2 * n_expert, cap, -1), WIDE).reshape(
            2 * slots, -1
        )

    arrived = [ring_gather(send_rows(tokens[:, h * cols : (h + 1) * cols])) for h in range(HALVES)]
    logits = jnp.dot(tokens, w_router, preferred_element_type=F32)
    expert_hot = one_hot.reshape(rows, 2, n_expert).astype(F32)
    chosen = jnp.sum(expert_hot * logits[:, None, :], axis=2)
    gate_first = jax.nn.sigmoid(chosen[:, 0] - chosen[:, 1])
    gate_weights = jnp.stack([gate_first, 1.0 - gate_first], axis=1)
    mixing = jnp.sum(gate_weights[:, :, None] * slot_pairs, axis=1)
    keys = substation_ids * HOURS + hour_index
    key_slot = jnp.sum(placing * keys.astype(F32)[:, None], axis=0)
    gate_slot = jnp.sum(mixing, axis=0)
    lane = lax.broadcasted_iota(jnp.int32, (slots, 128), 1)
    meta = jnp.where(lane == 0, key_slot[:, None], gate_slot[:, None])
    meta = jnp.broadcast_to(
        meta.reshape(n_expert, 1, cap, 128), (n_expert, 2, cap, 128)
    ).reshape(2 * n_expert, cap, 128)
    meta_rows = ring_gather(exchange(meta, WIDE).reshape(2 * slots, 128))

    hidden = []
    for b in range(5):
        acc = 0.0
        for h in range(HALVES):
            acc = acc + jnp.dot(
                arrived[h][b], up_local[h * cols : (h + 1) * cols], preferred_element_type=F32
            )
        hidden.append(jax.nn.gelu(acc).astype(BF))
    hidden_far = jnp.concatenate(hidden[3:], axis=0)

    returned = []
    for h in range(HALVES):
        w = down_local[:, h * cols : (h + 1) * cols]
        far, prev, nxt, own = [
            jnp.dot(v, w, preferred_element_type=F32).astype(BF).astype(F32)
            for v in (hidden_far, hidden[1], hidden[2], hidden[0])
        ]
        total = ring_scatter(own, prev, nxt, far)
        home = exchange(total.reshape(2 * n_expert, cap, cols), WIDE)
        home = home.reshape(n_expert, 2, cap, cols).astype(F32)
        returned.append((home[:, 0] + home[:, 1]).reshape(slots, cols))
    combined = jnp.concatenate(
        [jnp.dot(mixing, r, precision=lax.Precision.HIGHEST) for r in returned], axis=1
    )
    mixed = tokens.astype(F32) + combined

    mixed_b = mixed.astype(BF)
    mixed_rows = [ring_gather(send_rows(mixed_b[:, h * cols : (h + 1) * cols])) for h in range(HALVES)]

    rscale = 1.0 / jnp.sqrt(jnp.mean(mixed * mixed, axis=1, keepdims=True) + 1e-05)
    normed = (mixed * rscale * norm_gain[None, :]).astype(BF)
    loads = jnp.dot(normed, readout, preferred_element_type=F32)
    n_keys = target.shape[0]
    key_rows = n_keys // n_all
    key_hot = (keys[None, :] == jnp.arange(n_keys, dtype=jnp.int32)[:, None]).astype(F32)
    partial_table = jnp.dot(key_hot, loads, precision=lax.Precision.HIGHEST)
    table_own = jnp.sum(exchange(partial_table.reshape(n_all, key_rows, -1), ALL), axis=0)
    owner_start = lax.axis_index(ALL) * key_rows
    diff_own = table_own - lax.dynamic_slice_in_dim(target, owner_start, key_rows, 0)
    diff_send = jnp.broadcast_to(diff_own.astype(BF)[None], (n_all, key_rows, target.shape[1]))
    diff_all = exchange(diff_send, ALL).reshape(n_keys, -1)
    diff_f = diff_all.astype(F32)
    loss_value = 0.5 * jnp.mean(diff_f * diff_f)

    grad = 0.0
    for b in range(5):
        m = jnp.concatenate([mixed_rows[h][b] for h in range(HALVES)], axis=1).astype(F32)
        key_r = meta_rows[b][:, 0:1].astype(jnp.int32)
        gate_r = meta_rows[b][:, 1:2]
        hot = (key_r == lax.broadcasted_iota(jnp.int32, (key_r.shape[0], n_keys), 1)).astype(BF)
        g_loads = jnp.dot(hot, diff_all, preferred_element_type=F32).astype(BF)
        g_normed = lax.dot_general(
            g_loads, readout, (((1,), (1,)), ((), ())), preferred_element_type=F32
        )
        u = g_normed * norm_gain[None, :]
        rs = 1.0 / jnp.sqrt(jnp.mean(m * m, axis=1, keepdims=True) + 1e-05)
        g_mixed = rs * u - rs**3 * m * jnp.mean(u * m, axis=1, keepdims=True)
        g_out = (gate_r * g_mixed).astype(BF)
        grad = grad + lax.dot_general(
            hidden[b], g_out, (((0,), (0,)), ((), ())), preferred_element_type=F32
        )
    grad_down = grad.astype(BF)[None]
    return (table_own, loss_value, grad_down)


def solution(mesh):
    fine = Mesh(mesh.devices.reshape(4, 4, 2, 2, 4), ALL)
    placed = (
        P(ALL, None),
        P(),
        P(EXP, None, DP),
        P(EXP, DP, None),
        P(),
        P(),
        P(ALL, None),
        P(ALL),
        P(ALL),
        P(),
    )
    return jax.shard_map(
        local,
        mesh=fine,
        in_specs=placed,
        out_specs=(P(ALL, None), P(), P(EXP, DP, None)),
        check_vma=False,
    )
```

```python
import functools

import jax
import jax.numpy as jnp
from jax import lax
from jax.experimental import pallas as pl
from jax.experimental.pallas import tpu as pltpu
from jax.sharding import Mesh, PartitionSpec as P


HOURS = 8
BF = jnp.bfloat16
F32 = jnp.float32
EXP = ("zl", "x", "c")
WIDE = ("zl", "x", "c", "zh")
DP = ("zh", "y")
ALL = ("zl", "x", "c", "zh", "y")
BLOCK = 256
PIECE = 128


def exchange(x, axes):
    return lax.all_to_all(x, axes, split_axis=0, concat_axis=0, tiled=True)


def up_one(x):
    return lax.ppermute(x, "y", [(i, (i + 1) % 4) for i in range(4)])


def down_one(x):
    return lax.ppermute(x, "y", [(i, (i + 3) % 4) for i in range(4)])


def z_swap(x):
    return lax.ppermute(x, "zh", [(0, 1), (1, 0)])


def ring_gather(own, upward):
    prev = up_one(own)
    nxt = down_one(own)
    far = up_one(prev) if upward else down_one(nxt)
    return [own, prev, nxt, far]


def ring_scatter(blocks, upward):
    own, prev, nxt, far = blocks
    if upward:
        got = up_one(far)
        from_next = down_one(prev)
        from_prev = up_one((nxt.astype(F32) + got.astype(F32)).astype(BF))
    else:
        got = down_one(far)
        from_prev = up_one(nxt)
        from_next = down_one((prev.astype(F32) + got.astype(F32)).astype(BF))
    return own.astype(F32) + from_prev.astype(F32) + from_next.astype(F32)


def spread(own):
    halves = [own[:PIECE], own[PIECE:]]
    away = [z_swap(v) for v in halves]
    near = [ring_gather(v, n == 0) for n, v in enumerate(halves)]
    other = [ring_gather(v, n == 0) for n, v in enumerate(away)]
    return near[0] + near[1], other[0] + other[1]


def up_kernel(n_blocks, *refs):
    block_refs = refs[:n_blocks]
    w_ref, hidden_ref, turned_ref, meta_ref, rows_buf, sems = refs[n_blocks:]
    step = pl.program_id(0)
    per = hidden_ref.shape[0] // PIECE

    @pl.when(step == 0)
    def _():
        for k in range(n_blocks):
            pltpu.make_async_copy(
                block_refs[k], rows_buf.at[pl.ds(k * PIECE, PIECE), :], sems.at[k]
            ).start()

    for j in range(per):
        k = step * per + j
        pltpu.make_async_copy(
            block_refs[0],
            rows_buf.at[pl.ds(pl.multiple_of(k * PIECE, PIECE), PIECE), :],
            sems.at[k],
        ).wait()
    n_rows, width = hidden_ref.shape[0], w_ref.shape[0]
    here = pl.ds(pl.multiple_of(step * n_rows, n_rows), n_rows)
    acc = jnp.dot(rows_buf[here, :width], w_ref[...], preferred_element_type=F32)
    hidden = jax.nn.gelu(acc).astype(BF)
    hidden_ref[...] = hidden
    turned_ref[...] = hidden.T
    meta_ref[...] = rows_buf[here, width:]


def up_project(blocks, w):
    n_rows, width = len(blocks) * PIECE, blocks[0].shape[1]
    tile = 512
    return pl.pallas_call(
        functools.partial(up_kernel, len(blocks)),
        grid=(n_rows // tile,),
        out_shape=(
            jax.ShapeDtypeStruct((n_rows, w.shape[1]), BF),
            jax.ShapeDtypeStruct((w.shape[1], n_rows), BF),
            jax.ShapeDtypeStruct((n_rows, width - w.shape[0]), BF),
        ),
        in_specs=[pl.BlockSpec(memory_space=pl.ANY)] * len(blocks)
        + [pl.BlockSpec(w.shape, lambda i: (0, 0), pipeline_mode=pl.Buffered(1))],
        out_specs=(
            pl.BlockSpec((tile, w.shape[1]), lambda i: (i, 0)),
            pl.BlockSpec((w.shape[1], tile), lambda i: (0, i)),
            pl.BlockSpec((tile, width - w.shape[0]), lambda i: (i, 0)),
        ),
        scratch_shapes=[
            pltpu.VMEM((n_rows, width), BF),
            pltpu.SemaphoreType.DMA((len(blocks),)),
        ],
        compiler_params=pltpu.CompilerParams(vmem_limit_bytes=32 << 20),
        cost_estimate=pl.CostEstimate(
            flops=2 * n_rows * w.shape[0] * w.shape[1],
            bytes_accessed=2 * (n_rows * width + w.shape[0] * w.shape[1]),
            transcendentals=n_rows * w.shape[1],
        ),
        name="up_project",
    )(*blocks, w)


def down_kernel(hidden_ref, w_ref, *out_refs):
    part = jnp.dot(hidden_ref[...], w_ref[...], preferred_element_type=F32).astype(BF)
    for k, out in enumerate(out_refs):
        out[...] = part[k * PIECE : (k + 1) * PIECE]


def down_project(hidden, w):
    n_rows, n_hidden = hidden.shape
    width, tile = w.shape[1], 256
    n_blocks = n_rows // PIECE
    return pl.pallas_call(
        down_kernel,
        grid=(width // tile,),
        out_shape=[jax.ShapeDtypeStruct((PIECE, width), BF)] * n_blocks,
        in_specs=[
            pl.BlockSpec(hidden.shape, lambda i: (0, 0), pipeline_mode=pl.Buffered(1)),
            pl.BlockSpec((n_hidden, tile), lambda i: (0, i)),
        ],
        out_specs=[pl.BlockSpec((PIECE, tile), lambda i: (0, i))] * n_blocks,
        compiler_params=pltpu.CompilerParams(vmem_limit_bytes=24 << 20),
        cost_estimate=pl.CostEstimate(
            flops=2 * n_rows * n_hidden * width,
            bytes_accessed=2 * (n_rows * (n_hidden + width) + n_hidden * width),
            transcendentals=0,
        ),
        name="down_project",
    )(hidden, w)


def after(value, *others):
    return lax.optimization_barrier((value,) + others)[0]


def peers(x):
    out = [x]
    for b in range(1, 4):
        out.append(lax.ppermute(x, "y", [(i, (i - b) % 4) for i in range(4)]))
    return out


def backward_kernel(n_arrays, n_diffs, n_turned, *refs):
    meta_ref, readout_ref, gain_ref = refs[:3]
    diff_refs, refs = refs[3 : 3 + n_diffs], refs[3 + n_diffs :]
    turned_refs, refs = refs[:n_turned], refs[n_turned:]
    mixed_refs, refs = refs[:n_arrays], refs[n_arrays:]
    out_ref, rows_buf, hidden_buf, diff_buf, sems, diff_sems, hidden_sems = refs
    per = BLOCK // PIECE
    n_blocks = n_arrays // per
    step = pl.program_id(0)
    n_diff, n_turn = diff_refs[0].shape[0], turned_refs[0].shape[1]
    diff_copies = [
        pltpu.make_async_copy(
            diff_refs[j], diff_buf.at[pl.ds(j * n_diff, n_diff), :], diff_sems.at[j]
        )
        for j in range(n_diffs)
    ]
    hidden_copies = [
        pltpu.make_async_copy(
            turned_refs[j], hidden_buf.at[:, pl.ds(j * n_turn, n_turn)], hidden_sems.at[j]
        )
        for j in range(n_turned)
    ]

    @pl.when(step == 0)
    def _():
        for copy in diff_copies:
            copy.start()
        for k in range(n_arrays):
            pltpu.make_async_copy(
                mixed_refs[k], rows_buf.at[pl.ds(k * PIECE, PIECE), :], sems.at[k]
            ).start()
        for copy in hidden_copies:
            copy.start()
        for copy in diff_copies:
            copy.wait()

    @pl.when(step < n_blocks)
    def _():
        here = pl.ds(pl.multiple_of(step * BLOCK, BLOCK), BLOCK)
        pos = meta_ref[:, 0:1].astype(jnp.int32)
        gate = meta_ref[:, 1:2]
        n_keys = diff_buf.shape[0]
        hot = (pos == lax.broadcasted_iota(jnp.int32, (BLOCK, n_keys), 1)).astype(F32).astype(BF)
        g_loads = jnp.dot(hot, diff_buf[...], preferred_element_type=F32).astype(BF)
        g_normed = lax.dot_general(
            g_loads, readout_ref[...], (((1,), (1,)), ((), ())), preferred_element_type=F32
        )
        u = g_normed * gain_ref[...]
        for j in range(per):
            k = step * per + j
            pltpu.make_async_copy(
                mixed_refs[0],
                rows_buf.at[pl.ds(pl.multiple_of(k * PIECE, PIECE), PIECE), :],
                sems.at[k],
            ).wait()
        m = rows_buf[here, :].astype(F32)
        width = m.shape[1]
        square = jnp.sum(m * m, axis=1, keepdims=True) / width
        cross = jnp.sum(u * m, axis=1, keepdims=True) / width
        rs = 1.0 / jnp.sqrt(square + 1e-05)
        g_mixed = rs * u - (rs * rs * rs * cross) * m
        rows_buf[here, :] = (gate * g_mixed).astype(BF)

    @pl.when(step == n_blocks)
    def _():
        for copy in hidden_copies:
            copy.wait()

    @pl.when(step >= n_blocks)
    def _():
        size = out_ref.shape[1]
        cols = pl.ds(pl.multiple_of((step - n_blocks) * size, size), size)
        out_ref[...] = jnp.dot(
            hidden_buf[...], rows_buf[:, cols], preferred_element_type=F32
        ).astype(BF)


def backward(meta, readout, gain, diffs, turned, arrays):
    n_rows, width = meta.shape[0], gain.shape[1]
    n_hidden = turned[0].shape[0]
    out_cols = 256
    n_blocks = n_rows // BLOCK
    whole = lambda x: pl.BlockSpec(x.shape, lambda i: (0, 0))
    return pl.pallas_call(
        functools.partial(backward_kernel, len(arrays), len(diffs), len(turned)),
        grid=(n_blocks + width // out_cols,),
        out_shape=jax.ShapeDtypeStruct((n_hidden, width), BF),
        in_specs=[
            pl.BlockSpec((BLOCK, 128), lambda i: (jnp.minimum(i, n_blocks - 1), 0)),
            whole(readout),
            whole(gain),
        ]
        + [pl.BlockSpec(memory_space=pl.ANY)] * (len(diffs) + len(turned) + len(arrays)),
        out_specs=pl.BlockSpec((n_hidden, out_cols), lambda i: (0, jnp.maximum(i - n_blocks, 0))),
        scratch_shapes=[
            pltpu.VMEM((n_rows, width), BF),
            pltpu.VMEM((n_hidden, n_rows), BF),
            pltpu.VMEM((sum(d.shape[0] for d in diffs), 128), BF),
            pltpu.SemaphoreType.DMA((len(arrays),)),
            pltpu.SemaphoreType.DMA((len(diffs),)),
            pltpu.SemaphoreType.DMA((len(turned),)),
        ],
        compiler_params=pltpu.CompilerParams(vmem_limit_bytes=40 << 20),
        cost_estimate=pl.CostEstimate(
            flops=2 * n_rows * width * (n_hidden + 256),
            bytes_accessed=2 * n_rows * (width + n_hidden),
            transcendentals=0,
        ),
        name="backward",
    )(meta, readout, gain, *diffs, *turned, *arrays)


def local(
    tokens,
    w_router,
    w_up,
    w_down,
    norm_gain,
    readout,
    expert_ids,
    substation_ids,
    hour_index,
    target,
):
    n_expert = 32
    rows, width = tokens.shape
    cap = 2 * rows // n_expert
    slots = n_expert * cap
    up_local, down_local = w_up[0], w_down[0]
    flat_expert = expert_ids.reshape(-1)
    one_hot = (flat_expert[:, None] == jnp.arange(n_expert, dtype=jnp.int32)[None, :]).astype(
        jnp.int32
    )
    position = jnp.sum((jnp.cumsum(one_hot, axis=0) - 1) * one_hot, axis=1)
    slot_index = flat_expert * cap + position
    slot_hot = (slot_index[:, None] == jnp.arange(slots, dtype=jnp.int32)[None, :]).astype(F32)
    slot_pairs = slot_hot.reshape(rows, 2, slots)
    placing = jnp.sum(slot_pairs, axis=1)
    placing_b = placing.astype(BF)

    def send(values):
        got = lax.dot_general(
            placing_b, values, (((0,), (0,)), ((), ())), preferred_element_type=F32
        )
        return exchange(got.astype(BF).reshape(n_expert, cap, -1), EXP).reshape(slots, -1)

    logits = jnp.dot(tokens, w_router, preferred_element_type=F32)
    expert_hot = one_hot.reshape(rows, 2, n_expert).astype(F32)
    chosen = jnp.sum(expert_hot * logits[:, None, :], axis=2)
    gate_first = jax.nn.sigmoid(chosen[:, 0] - chosen[:, 1])
    gate_weights = jnp.stack([gate_first, 1.0 - gate_first], axis=1)
    mixing = jnp.sum(gate_weights[:, :, None] * slot_pairs, axis=1)
    keys = substation_ids * HOURS + hour_index
    lane = lax.broadcasted_iota(jnp.int32, (rows, 128), 1)
    gate_a = lax.reduce_precision(gate_first, 8, 7)
    gate_b = lax.reduce_precision(gate_first - gate_a, 8, 7)
    gate_c = gate_first - gate_a - gate_b
    meta = jnp.zeros((rows, 128), F32)
    for n, v in enumerate(
        (substation_ids, hour_index, expert_ids[:, 0], gate_a, gate_b, gate_c)
    ):
        meta = jnp.where(lane == n, v.astype(F32)[:, None], meta)

    tokens_meta = jnp.concatenate([tokens, meta.astype(BF)], axis=1)
    near, other = spread(send(tokens_meta))

    hidden_near, turned_near, meta_near = up_project(near, up_local)
    part_near = down_project(hidden_near, down_local)
    hidden_other, turned_other, meta_other = up_project(other, up_local)
    meta_rows = jnp.concatenate([meta_near, meta_other], axis=0).astype(F32)
    part_other = down_project(hidden_other, down_local)
    total = []
    crossed = [
        z_swap(ring_scatter(part_other[4 * n : 4 * n + 4], n == 0).astype(BF))
        for n in range(2)
    ]
    for n in range(2):
        near_sum = ring_scatter(part_near[4 * n : 4 * n + 4], n == 0)
        total.append((near_sum + crossed[n].astype(F32)).astype(BF))
    total = jnp.concatenate(total, axis=0)
    returned = exchange(total.reshape(n_expert, cap, width), EXP).reshape(slots, width)
    combined = jnp.dot(mixing, returned.astype(F32), precision=lax.Precision.HIGHEST)
    mixed = tokens.astype(F32) + combined
    mixed_b = mixed.astype(BF)

    last = send(mixed_b)
    near, other = spread(last)
    mixed_rows = near + other

    rscale = 1.0 / jnp.sqrt(jnp.mean(mixed * mixed, axis=1, keepdims=True) + 1e-05)
    normed = (mixed * rscale * norm_gain[None, :]).astype(BF)
    loads = jnp.dot(normed, readout, preferred_element_type=F32)
    key_row = jnp.broadcast_to(keys.astype(F32)[None, :], (8, rows))
    groups = peers(jnp.concatenate([loads, key_row], axis=0))
    y = lax.axis_index("y")
    n_keys = target.shape[0]
    per_y = n_keys // 4
    k = jnp.concatenate([g[rows] for g in groups]).astype(jnp.int32)
    row = jnp.where((k >> 3) % 4 == y, (k >> 5) * 8 + k % 8, -1)
    hot = (row[None, :] == jnp.arange(per_y, dtype=jnp.int32)[:, None]).astype(BF)
    values = jnp.concatenate([g[:rows] for g in groups], axis=0)
    high = lax.reduce_precision(values, 8, 7)
    both = jnp.concatenate([high.astype(BF), (values - high).astype(BF)], axis=1)
    sums = jnp.dot(hot, both, preferred_element_type=F32)
    table_part = (sums[:, :128] + sums[:, 128:]).astype(BF)
    table_part = after(table_part.reshape(2 * n_expert, 8, -1), last)
    table_pieces = exchange(table_part, WIDE)
    table_own = jnp.sum(table_pieces.astype(F32), axis=0)
    owner_start = lax.axis_index(ALL) * 8
    diff_own = table_own - lax.dynamic_slice_in_dim(target, owner_start, 8, 0)

    diff_send = jnp.broadcast_to(diff_own.astype(BF)[None], (2 * n_expert, 8, target.shape[1]))
    diffs = peers(exchange(diff_send, WIDE).reshape(per_y, -1))
    loss_value = sum(jnp.sum(jnp.square(d.astype(F32))) for d in diffs) * (
        0.5 / (n_keys * target.shape[1])
    )

    k = (meta_rows[:, 0:1] * HOURS + meta_rows[:, 1:2]).astype(jnp.int32)
    pos = (((k >> 3) - y) % 4) * per_y + (k >> 5) * 8 + k % 8
    gate = meta_rows[:, 3:4] + meta_rows[:, 4:5] + meta_rows[:, 5:6]
    is_first = meta_rows[:, 2:3].astype(jnp.int32) == lax.axis_index(EXP)
    gate = jnp.where(is_first, gate, 1.0 - gate)
    lane = lax.broadcasted_iota(jnp.int32, meta_rows.shape, 1)
    meta_pos = jnp.where(lane == 0, pos.astype(F32), gate)
    grad_down = backward(meta_pos, readout, norm_gain[None, :], diffs, (turned_near, turned_other), mixed_rows)[None]
    return (table_own, loss_value, grad_down)


def solution(mesh):
    fine = Mesh(mesh.devices.reshape(4, 4, 2, 2, 4), ALL)
    placed = (
        P(ALL, None),
        P(),
        P(EXP, None, DP),
        P(EXP, DP, None),
        P(),
        P(),
        P(ALL, None),
        P(ALL),
        P(ALL),
        P(),
    )
    return jax.shard_map(
        local,
        mesh=fine,
        in_specs=placed,
        out_specs=(P(ALL, None), P(), P(EXP, DP, None)),
        check_vma=False,
    )
```

```python
import functools

import jax
import jax.numpy as jnp
from jax import lax
from jax.experimental import pallas as pl
from jax.experimental.pallas import tpu as pltpu
from jax.sharding import Mesh, PartitionSpec as P


HOURS = 8
BF = jnp.bfloat16
F32 = jnp.float32
EXP = ("zl", "x", "c")
WIDE = ("zl", "x", "c", "zh")
DP = ("zh", "y")
ALL = ("zl", "x", "c", "zh", "y")
BLOCK = 256
PIECE = 128


def exchange(x, axes):
    return lax.all_to_all(x, axes, split_axis=0, concat_axis=0, tiled=True)


def up_one(x):
    return lax.ppermute(x, "y", [(i, (i + 1) % 4) for i in range(4)])


def down_one(x):
    return lax.ppermute(x, "y", [(i, (i + 3) % 4) for i in range(4)])


def z_swap(x):
    return lax.ppermute(x, "zh", [(0, 1), (1, 0)])


def ring_gather(own, upward):
    prev = up_one(own)
    nxt = down_one(own)
    far = up_one(prev) if upward else down_one(nxt)
    return [own, prev, nxt, far]


def ring_scatter(blocks, upward):
    own, prev, nxt, far = blocks
    if upward:
        got = up_one(far)
        from_next = down_one(prev)
        from_prev = up_one((nxt.astype(F32) + got.astype(F32)).astype(BF))
    else:
        got = down_one(far)
        from_prev = up_one(nxt)
        from_next = down_one((prev.astype(F32) + got.astype(F32)).astype(BF))
    return own.astype(F32) + from_prev.astype(F32) + from_next.astype(F32)


def spread(own):
    halves = [own[:PIECE], own[PIECE:]]
    away = [z_swap(v) for v in halves]
    near = [ring_gather(v, n == 0) for n, v in enumerate(halves)]
    other = [ring_gather(v, n == 0) for n, v in enumerate(away)]
    return near[0] + near[1], other[0], other[1]


def up_kernel(n_blocks, *refs):
    block_refs = refs[:n_blocks]
    w_ref, hidden_ref, turned_ref, meta_ref, rows_buf, sems = refs[n_blocks:]
    step = pl.program_id(0)
    per = hidden_ref.shape[0] // PIECE

    @pl.when(step == 0)
    def _():
        for k in range(n_blocks):
            pltpu.make_async_copy(
                block_refs[k], rows_buf.at[pl.ds(k * PIECE, PIECE), :], sems.at[k]
            ).start()

    for j in range(per):
        k = step * per + j
        pltpu.make_async_copy(
            block_refs[0],
            rows_buf.at[pl.ds(pl.multiple_of(k * PIECE, PIECE), PIECE), :],
            sems.at[k],
        ).wait()
    n_rows, width = hidden_ref.shape[0], w_ref.shape[0]
    here = pl.ds(pl.multiple_of(step * n_rows, n_rows), n_rows)
    acc = jnp.dot(rows_buf[here, :width], w_ref[...], preferred_element_type=F32)
    hidden = jax.nn.gelu(acc).astype(BF)
    hidden_ref[...] = hidden
    turned_ref[...] = hidden.T
    meta_ref[...] = rows_buf[here, width:]


def up_project(blocks, w):
    n_rows, width = len(blocks) * PIECE, blocks[0].shape[1]
    tile = 512
    return pl.pallas_call(
        functools.partial(up_kernel, len(blocks)),
        grid=(n_rows // tile,),
        out_shape=(
            jax.ShapeDtypeStruct((n_rows, w.shape[1]), BF),
            jax.ShapeDtypeStruct((w.shape[1], n_rows), BF),
            jax.ShapeDtypeStruct((n_rows, width - w.shape[0]), BF),
        ),
        in_specs=[pl.BlockSpec(memory_space=pl.ANY)] * len(blocks)
        + [pl.BlockSpec(w.shape, lambda i: (0, 0), pipeline_mode=pl.Buffered(1))],
        out_specs=(
            pl.BlockSpec((tile, w.shape[1]), lambda i: (i, 0)),
            pl.BlockSpec((w.shape[1], tile), lambda i: (0, i)),
            pl.BlockSpec((tile, width - w.shape[0]), lambda i: (i, 0)),
        ),
        scratch_shapes=[
            pltpu.VMEM((n_rows, width), BF),
            pltpu.SemaphoreType.DMA((len(blocks),)),
        ],
        compiler_params=pltpu.CompilerParams(vmem_limit_bytes=32 << 20),
        cost_estimate=pl.CostEstimate(
            flops=2 * n_rows * w.shape[0] * w.shape[1],
            bytes_accessed=2 * (n_rows * width + w.shape[0] * w.shape[1]),
            transcendentals=n_rows * w.shape[1],
        ),
        name="up_project",
    )(*blocks, w)


def down_kernel(hidden_ref, w_ref, *out_refs):
    part = jnp.dot(hidden_ref[...], w_ref[...], preferred_element_type=F32).astype(BF)
    for k, out in enumerate(out_refs):
        out[...] = part[k * PIECE : (k + 1) * PIECE]


def down_project(hidden, w):
    n_rows, n_hidden = hidden.shape
    width, tile = w.shape[1], 256
    n_blocks = n_rows // PIECE
    return pl.pallas_call(
        down_kernel,
        grid=(width // tile,),
        out_shape=[jax.ShapeDtypeStruct((PIECE, width), BF)] * n_blocks,
        in_specs=[
            pl.BlockSpec(hidden.shape, lambda i: (0, 0), pipeline_mode=pl.Buffered(1)),
            pl.BlockSpec((n_hidden, tile), lambda i: (0, i)),
        ],
        out_specs=[pl.BlockSpec((PIECE, tile), lambda i: (0, i))] * n_blocks,
        compiler_params=pltpu.CompilerParams(vmem_limit_bytes=24 << 20),
        cost_estimate=pl.CostEstimate(
            flops=2 * n_rows * n_hidden * width,
            bytes_accessed=2 * (n_rows * (n_hidden + width) + n_hidden * width),
            transcendentals=0,
        ),
        name="down_project",
    )(hidden, w)


def after(value, *others):
    return lax.optimization_barrier((value,) + others)[0]


def peers(x):
    out = [x]
    for b in range(1, 4):
        out.append(lax.ppermute(x, "y", [(i, (i - b) % 4) for i in range(4)]))
    return out


def backward_kernel(n_arrays, n_diffs, n_turned, *refs):
    meta_ref, weights_ref = refs[:2]
    diff_refs, refs = refs[2 : 2 + n_diffs], refs[2 + n_diffs :]
    turned_refs, refs = refs[:n_turned], refs[n_turned:]
    mixed_refs, refs = refs[:n_arrays], refs[n_arrays:]
    out_ref, rows_buf, hidden_buf, diff_buf, sems, diff_sems, hidden_sems = refs
    per = BLOCK // PIECE
    n_blocks = n_arrays // per
    step = pl.program_id(0)
    n_diff = diff_refs[0].shape[0]
    starts = [sum(r.shape[1] for r in turned_refs[:j]) for j in range(n_turned)]
    diff_copies = [
        pltpu.make_async_copy(
            diff_refs[j], diff_buf.at[pl.ds(j * n_diff, n_diff), :], diff_sems.at[j]
        )
        for j in range(n_diffs)
    ]
    hidden_copies = [
        pltpu.make_async_copy(
            turned_refs[j],
            hidden_buf.at[:, pl.ds(starts[j], turned_refs[j].shape[1])],
            hidden_sems.at[j],
        )
        for j in range(n_turned)
    ]

    @pl.when(step == 0)
    def _():
        for copy in diff_copies:
            copy.start()
        for k in range(n_arrays):
            pltpu.make_async_copy(
                mixed_refs[k], rows_buf.at[pl.ds(k * PIECE, PIECE), :], sems.at[k]
            ).start()
        for copy in hidden_copies:
            copy.start()
        for copy in diff_copies:
            copy.wait()

    @pl.when(step < n_blocks)
    def _():
        here = pl.ds(pl.multiple_of(step * BLOCK, BLOCK), BLOCK)
        pos = meta_ref[:, 0:1].astype(jnp.int32)
        gate = meta_ref[:, 1:2]
        n_keys = diff_buf.shape[0]
        hot = (pos == lax.broadcasted_iota(jnp.int32, (BLOCK, n_keys), 1)).astype(F32).astype(BF)
        g_loads = jnp.dot(hot, diff_buf[...], preferred_element_type=F32).astype(BF)
        u = lax.dot_general(
            jnp.concatenate([g_loads, g_loads], axis=1),
            weights_ref[...],
            (((1,), (1,)), ((), ())),
            preferred_element_type=F32,
        )
        for j in range(per):
            k = step * per + j
            pltpu.make_async_copy(
                mixed_refs[0],
                rows_buf.at[pl.ds(pl.multiple_of(k * PIECE, PIECE), PIECE), :],
                sems.at[k],
            ).wait()
        m = rows_buf[here, :].astype(F32)
        width = m.shape[1]
        square = jnp.sum(m * m, axis=1, keepdims=True) / width
        cross = jnp.sum(u * m, axis=1, keepdims=True) / width
        rs = 1.0 / jnp.sqrt(square + 1e-05)
        near_scale = gate * rs
        rows_buf[here, :] = (near_scale * u - (near_scale * rs * rs * cross) * m).astype(BF)

    @pl.when(step == n_blocks)
    def _():
        for copy in hidden_copies:
            copy.wait()

    @pl.when(step >= n_blocks)
    def _():
        size = out_ref.shape[1]
        cols = pl.ds(pl.multiple_of((step - n_blocks) * size, size), size)
        out_ref[...] = jnp.dot(
            hidden_buf[...], rows_buf[:, cols], preferred_element_type=F32
        ).astype(BF)


def backward(meta, weights, diffs, turned, arrays):
    n_rows, width = meta.shape[0], weights.shape[0]
    n_hidden = turned[0].shape[0]
    out_cols = 256
    n_blocks = n_rows // BLOCK
    whole = lambda x: pl.BlockSpec(x.shape, lambda i: (0, 0))
    return pl.pallas_call(
        functools.partial(backward_kernel, len(arrays), len(diffs), len(turned)),
        grid=(n_blocks + width // out_cols,),
        out_shape=jax.ShapeDtypeStruct((n_hidden, width), BF),
        in_specs=[
            pl.BlockSpec((BLOCK, 128), lambda i: (jnp.minimum(i, n_blocks - 1), 0)),
            whole(weights),
        ]
        + [pl.BlockSpec(memory_space=pl.ANY)] * len(diffs)
        + [pl.BlockSpec(memory_space=pltpu.HBM)] * len(turned)
        + [pl.BlockSpec(memory_space=pl.ANY)] * len(arrays),
        out_specs=pl.BlockSpec((n_hidden, out_cols), lambda i: (0, jnp.maximum(i - n_blocks, 0))),
        scratch_shapes=[
            pltpu.VMEM((n_rows, width), BF),
            pltpu.VMEM((n_hidden, n_rows), BF),
            pltpu.VMEM((sum(d.shape[0] for d in diffs), 128), BF),
            pltpu.SemaphoreType.DMA((len(arrays),)),
            pltpu.SemaphoreType.DMA((len(diffs),)),
            pltpu.SemaphoreType.DMA((len(turned),)),
        ],
        compiler_params=pltpu.CompilerParams(vmem_limit_bytes=40 << 20),
        cost_estimate=pl.CostEstimate(
            flops=2 * n_rows * width * (n_hidden + 256),
            bytes_accessed=2 * n_rows * (width + n_hidden),
            transcendentals=0,
        ),
        name="backward",
    )(meta, weights, *diffs, *turned, *arrays)


def local(
    tokens,
    w_router,
    w_up,
    w_down,
    norm_gain,
    readout,
    expert_ids,
    substation_ids,
    hour_index,
    target,
):
    n_expert = 32
    rows, width = tokens.shape
    cap = 2 * rows // n_expert
    slots = n_expert * cap
    up_local, down_local = w_up[0], w_down[0]
    flat_expert = expert_ids.reshape(-1)
    one_hot = (flat_expert[:, None] == jnp.arange(n_expert, dtype=jnp.int32)[None, :]).astype(
        jnp.int32
    )
    position = jnp.sum((jnp.cumsum(one_hot, axis=0) - 1) * one_hot, axis=1)
    slot_index = flat_expert * cap + position
    slot_hot = (slot_index[:, None] == jnp.arange(slots, dtype=jnp.int32)[None, :]).astype(F32)
    slot_pairs = slot_hot.reshape(rows, 2, slots)
    placing = jnp.sum(slot_pairs, axis=1)
    placing_b = placing.astype(BF)

    def send(values):
        got = lax.dot_general(
            placing_b, values, (((0,), (0,)), ((), ())), preferred_element_type=F32
        )
        return exchange(got.astype(BF).reshape(n_expert, cap, -1), EXP).reshape(slots, -1)

    logits = jnp.dot(tokens, w_router, preferred_element_type=F32)
    expert_hot = one_hot.reshape(rows, 2, n_expert).astype(F32)
    chosen = jnp.sum(expert_hot * logits[:, None, :], axis=2)
    gate_first = jax.nn.sigmoid(chosen[:, 0] - chosen[:, 1])
    gate_weights = jnp.stack([gate_first, 1.0 - gate_first], axis=1)
    mixing = jnp.sum(gate_weights[:, :, None] * slot_pairs, axis=1)
    keys = substation_ids * HOURS + hour_index
    lane = lax.broadcasted_iota(jnp.int32, (rows, 128), 1)
    gate_a = lax.reduce_precision(gate_first, 8, 7)
    gate_b = lax.reduce_precision(gate_first - gate_a, 8, 7)
    gate_c = gate_first - gate_a - gate_b
    meta = jnp.zeros((rows, 128), F32)
    for n, v in enumerate(
        (substation_ids, hour_index, expert_ids[:, 0], gate_a, gate_b, gate_c)
    ):
        meta = jnp.where(lane == n, v.astype(F32)[:, None], meta)

    tokens_meta = jnp.concatenate([tokens, meta.astype(BF)], axis=1)
    near, first, second = spread(send(tokens_meta))

    hidden_near, turned_near, meta_near = up_project(near, up_local)
    hidden_first, turned_first, meta_first = up_project(first, up_local)
    part_first = down_project(hidden_first, down_local)
    hidden_second, turned_second, meta_second = up_project(second, up_local)
    part_second = down_project(hidden_second, down_local)
    part_near = down_project(hidden_near, down_local)
    meta_rows = jnp.concatenate([meta_near, meta_first, meta_second], axis=0).astype(F32)
    part_other = [part_first, part_second]
    total = []
    crossed = [z_swap(ring_scatter(part_other[n], n == 0).astype(BF)) for n in range(2)]
    for n in range(2):
        near_sum = ring_scatter(part_near[4 * n : 4 * n + 4], n == 0)
        total.append((near_sum + crossed[n].astype(F32)).astype(BF))
    total = jnp.concatenate(total, axis=0)
    returned = exchange(total.reshape(n_expert, cap, width), EXP).reshape(slots, width)
    combined = jnp.dot(mixing, returned.astype(F32), precision=lax.Precision.HIGHEST)
    mixed = tokens.astype(F32) + combined
    mixed_b = mixed.astype(BF)

    last = send(mixed_b)
    mixed_rows = sum(spread(last), [])

    rscale = 1.0 / jnp.sqrt(jnp.mean(mixed * mixed, axis=1, keepdims=True) + 1e-05)
    normed = (mixed * rscale * norm_gain[None, :]).astype(BF)
    loads = jnp.dot(normed, readout, preferred_element_type=F32)
    key_row = jnp.broadcast_to(keys.astype(F32)[None, :], (8, rows))
    groups = peers(jnp.concatenate([loads, key_row], axis=0))
    y = lax.axis_index("y")
    n_keys = target.shape[0]
    per_y = n_keys // 4
    k = jnp.concatenate([g[rows] for g in groups]).astype(jnp.int32)
    row = jnp.where((k >> 3) % 4 == y, (k >> 5) * 8 + k % 8, -1)
    hot = (row[None, :] == jnp.arange(per_y, dtype=jnp.int32)[:, None]).astype(BF)
    values = jnp.concatenate([g[:rows] for g in groups], axis=0)
    high = lax.reduce_precision(values, 8, 7)
    both = jnp.concatenate([high.astype(BF), (values - high).astype(BF)], axis=1)
    sums = jnp.dot(hot, both, preferred_element_type=F32)
    table_part = (sums[:, :128] + sums[:, 128:]).astype(BF)
    table_part = after(table_part.reshape(2 * n_expert, 8, -1), last)
    table_pieces = exchange(table_part, WIDE)
    table_own = jnp.sum(table_pieces.astype(F32), axis=0)
    owner_start = lax.axis_index(ALL) * 8
    diff_own = table_own - lax.dynamic_slice_in_dim(target, owner_start, 8, 0)

    diff_send = jnp.broadcast_to(diff_own.astype(BF)[None], (2 * n_expert, 8, target.shape[1]))
    diffs = peers(exchange(diff_send, WIDE).reshape(per_y, -1))
    loss_value = sum(jnp.sum(jnp.square(d.astype(F32))) for d in diffs) * (
        0.5 / (n_keys * target.shape[1])
    )

    k = (meta_rows[:, 0:1] * HOURS + meta_rows[:, 1:2]).astype(jnp.int32)
    pos = (((k >> 3) - y) % 4) * per_y + (k >> 5) * 8 + k % 8
    gate = meta_rows[:, 3:4] + meta_rows[:, 4:5] + meta_rows[:, 5:6]
    is_first = meta_rows[:, 2:3].astype(jnp.int32) == lax.axis_index(EXP)
    gate = jnp.where(is_first, gate, 1.0 - gate)
    lane = lax.broadcasted_iota(jnp.int32, meta_rows.shape, 1)
    meta_pos = jnp.where(lane == 0, pos.astype(F32), gate)
    gained = readout.astype(F32) * norm_gain[:, None]
    high = lax.reduce_precision(gained, 8, 7)
    weights = jnp.concatenate([high.astype(BF), (gained - high).astype(BF)], axis=1)
    grad_down = backward(meta_pos, weights, diffs, (turned_near, turned_first, turned_second), mixed_rows)[None]
    return (table_own, loss_value, grad_down)


def solution(mesh):
    fine = Mesh(mesh.devices.reshape(4, 4, 2, 2, 4), ALL)
    placed = (
        P(ALL, None),
        P(),
        P(EXP, None, DP),
        P(EXP, DP, None),
        P(),
        P(),
        P(ALL, None),
        P(ALL),
        P(ALL),
        P(),
    )
    return jax.shard_map(
        local,
        mesh=fine,
        in_specs=placed,
        out_specs=(P(ALL, None), P(), P(EXP, DP, None)),
        check_vma=False,
    )
```
